32 devices in a mesh: seq: 8 (over y, x, core), seg: 4 (over z).
Axes of the slice: x: 2, y: 2, z: 4, core: 2. Of those that a mesh axis runs over, the one named last changes fastest.
Arguments:
- query_rows: bfloat16 [4, 2048, 4, 128], P('seg', 'seq'), may hold values from -6 to 6
- key_rows: bfloat16 [4, 2048, 2, 4, 128], P('seg', 'seq'), may hold values from -6 to 6
- value_rows: bfloat16 [4, 2048, 2, 4, 128], P('seg', 'seq'), may hold values from -6 to 6
- out_gain: float32 [4, 128], replicated, may hold values from 0.5 to 1.5
- initial_state: float32 [4, 128, 128], replicated, may hold values from -24 to 24
Outputs:
- normed_out: bfloat16 [4, 2048, 4, 128], P('seg', 'seq')
The draws below stay inside these ranges and needn't reach their ends.
All inputs are finite; a program needn't handle non-finite values.
Results may differ from the reference program's by a relative error of at most 0.004.
Values sent between devices are 32-bit elements; how exact they have to be, the bound alone decides.
A program may use at most 128 MiB of HBM per device.

```python
import jax
import jax.numpy as jnp
from jax import lax

DK = 128
DV = 128
HEADS = 4
REFL = 2
GROUP = 128
SEGTOK = 2048
SEGS = 4


def steps_of(key, shape, pieces, low, top_value):
    loudness = 1.0
    for position, shards_of in pieces:
        heights = jax.random.uniform(jax.random.fold_in(jax.random.fold_in(key, 6), position), (shards_of,), jnp.float32, low / len(pieces), top_value / len(pieces))
        loudness = loudness * jnp.repeat(jnp.exp(heights), shape[position] // shards_of).reshape((-1,) + (1,) * (len(shape) - 1 - position))
    return loudness


def normal_values(rng, dims, spread, reach, split=(), kind=jnp.bfloat16):
    values = jax.random.normal(rng, dims, jnp.float32) * spread
    if len(split) > 0:
        values = steps_of(rng, dims, split, -0.22, 0.18) * values
    return jnp.clip(values, min=-reach, max=reach).astype(kind)


def setup_inputs(seed: int = 0) -> dict:
    key_list = jax.random.split(jax.random.key(seed), 6)
    return {
        "query_rows": normal_values(key_list[0], (SEGS, SEGTOK, HEADS, DK), 1.0, 6.0, ((0, 4), (1, 8))),
        "key_rows": normal_values(key_list[1], (SEGS, SEGTOK, REFL, HEADS, DK), 1.0, 6.0, ((0, 4), (1, 8))),
        "value_rows": normal_values(key_list[2], (SEGS, SEGTOK, REFL, HEADS, DV), 1.0, 6.0, ((0, 4), (1, 8))),
        "out_gain": jnp.clip(1.0 + 0.1 * jax.random.normal(key_list[3], (HEADS, DV), jnp.float32), 0.5, 1.5),
        "initial_state": normal_values(key_list[4], (HEADS, DK, DV), 4.0, 24.0, (), jnp.float32),
    }


highest = lax.Precision.HIGHEST

def unit_keys(raw):
    raw = raw.astype(jnp.float32)
    return raw * lax.rsqrt(lax.optimization_barrier(jnp.sum(raw * raw, axis=-1, keepdims=True)) + 1e-06)

def solve_single(matrix, target):
    return jax.scipy.linalg.solve_triangular(matrix, target, lower=True, unit_diagonal=True)

def block_factors(query, keyed, valued):
    steps = keyed.shape[-2]
    tokens = query.shape[-2]
    key_gram = jnp.einsum('...id,...jd->...ij', keyed, keyed, precision=highest)
    lower_unit = jnp.eye(steps, dtype=jnp.float32) + jnp.tril(2.0 * key_gram, -1)
    target = jnp.concatenate([2.0 * keyed, 2.0 * valued], axis=-1)
    flat_lower = lower_unit.reshape(-1, steps, steps)
    flat_target = target.reshape(-1, steps, target.shape[-1])
    solved = jax.vmap(solve_single)(flat_lower, flat_target).reshape(target.shape)
    weights = solved[..., :keyed.shape[-1]]
    updates = solved[..., keyed.shape[-1]:]
    visible = jnp.arange(steps)[None, :] <= REFL * jnp.arange(tokens)[:, None] + (REFL - 1)
    scores = jnp.where(visible, jnp.einsum('...td,...ld->...tl', query, keyed, precision=highest), 0.0)
    return (weights, updates, scores)

def reference(query_rows, key_rows, value_rows, out_gain, initial_state):
    total = query_rows.shape[0] * query_rows.shape[1]
    nblock = total // GROUP
    query = query_rows.astype(jnp.float32).reshape(nblock, GROUP, HEADS, DK).transpose(0, 2, 1, 3)
    keyed = unit_keys(key_rows).reshape(nblock, GROUP * REFL, HEADS, DK).transpose(0, 2, 1, 3)
    valued = value_rows.astype(jnp.float32).reshape(nblock, GROUP * REFL, HEADS, DV).transpose(0, 2, 1, 3)

    def advance(state, block):
        query_block, key_block, value_block = block
        weights, updates, scores = block_factors(query_block, key_block, value_block)
        residue = updates - jnp.einsum('hld,hde->hle', weights, state, precision=highest)
        read = jnp.einsum('htd,hde->hte', query_block, state, precision=highest)
        read = read + jnp.einsum('htl,hle->hte', scores, residue, precision=highest)
        state = state + jnp.einsum('hld,hle->hde', key_block, residue, precision=highest)
        return (state, read)
    final_state, reads = lax.scan(advance, initial_state.astype(jnp.float32), (query, keyed, valued))
    reads = reads.transpose(0, 2, 1, 3).reshape(query_rows.shape[0], query_rows.shape[1], HEADS, DV)
    scale = lax.rsqrt(lax.optimization_barrier(jnp.mean(reads * reads, axis=-1, keepdims=True)) + 1e-06)
    return (reads * scale * out_gain).astype(jnp.bfloat16)
```

```python
import functools

import jax
import jax.numpy as jnp
from jax import lax
from jax.experimental import pallas as pl
from jax.experimental.pallas import tpu as pltpu
from jax.sharding import PartitionSpec as P

F32 = jnp.float32
BF16 = jnp.bfloat16
REFL = 2
BLK = 128
SUB = 16
MESH = pl.DeviceIdType.MESH


def dot(a, b):
    return lax.dot_general(a, b, (((1,), (0,)), ((), ())), preferred_element_type=F32)


def dot_bt(a, b):
    return lax.dot_general(a, b, (((1,), (1,)), ((), ())), preferred_element_type=F32)


def dot_at(a, b):
    return lax.dot_general(a, b, (((0,), (0,)), ((), ())), preferred_element_type=F32)


def split(x):
    high = x.astype(BF16)
    return high, (x - high.astype(F32)).astype(BF16)


def dot3(a, b):
    ah, al = a
    bh, bl = b
    return dot(ah, bh) + (dot(ah, bl) + dot(al, bh))


def iota(shape, axis):
    return lax.broadcasted_iota(jnp.int32, shape, axis)


def local_kernel(heads, q_ref, k_ref, v_ref, pair_ref, reach_ref, base_ref, dsc, nsc):
    steps = k_ref.shape[0]
    dk = q_ref.shape[1] // heads
    dv = v_ref.shape[1] // heads
    nblk = steps // BLK
    tok = BLK // REFL
    row, col = iota((BLK, BLK), 0), iota((BLK, BLK), 1)
    eye = row == col
    lane = iota((SUB, BLK), 1)
    chunks = [(h, c) for h in range(heads) for c in range(nblk)]
    count = len(chunks)

    keys, lowers, rcols, rrows = [], [], [], []
    for n, (h, c) in enumerate(chunks):
        key = k_ref[c * BLK : (c + 1) * BLK, h * dk : (h + 1) * dk]
        gram = dot_bt(key, key)
        diag = jnp.where(eye, gram, 0.0)
        rcol = lax.rsqrt(jnp.sum(diag, axis=1, keepdims=True) + 1e-6)
        rrow = lax.rsqrt(jnp.sum(diag, axis=0, keepdims=True) + 1e-6)
        lower = jnp.where(row > col, gram * (2.0 * rcol) * rrow, 0.0)
        packed = jnp.zeros((SUB, BLK), F32)
        for g in range(BLK // SUB):
            packed = jnp.where(lane // SUB == g, lower[g * SUB : (g + 1) * SUB], packed)
        dsc[n * SUB : (n + 1) * SUB, :] = packed
        keys.append(key)
        lowers.append(lower)
        rcols.append(rcol)
        rrows.append(rrow)

    lane_c = iota((count, BLK), 1)
    solved = []
    for i in range(SUB):
        line = dsc[pl.ds(i, count, stride=SUB), :]
        total = jnp.where(lane_c % SUB == i, 1.0, 0.0)
        for j in range(i):
            factor = jnp.take_along_axis(line, (lane_c // SUB) * SUB + j, axis=1)
            total = total - factor * solved[j]
        solved.append(total)
        nsc[pl.ds(i, count, stride=SUB), :] = total

    inverses = []
    for n in range(count):
        packed = nsc[n * SUB : (n + 1) * SUB, :]
        inverses.append(
            jnp.concatenate(
                [jnp.where(lane // SUB == g, packed, 0.0) for g in range(BLK // SUB)], axis=0
            )
        )
    size = SUB
    while size < BLK:
        mask = (row // size != col // size) & (row // (2 * size) == col // (2 * size))
        for n in range(count):
            inv = split(inverses[n])
            part = dot3(split(jnp.where(mask, lowers[n], 0.0)), inv)
            inverses[n] = inverses[n] - dot3(inv, split(part))
        size *= 2

    for h in range(heads):
        trans = add = None
        for c in range(nblk):
            n = h * nblk + c
            key, rcol, rrow = keys[n], rcols[n], rrows[n]
            value = v_ref[c * BLK : (c + 1) * BLK, h * dv : (h + 1) * dv]
            query = q_ref[c * tok : (c + 1) * tok, h * dk : (h + 1) * dk]
            nk = split(inverses[n] * (2.0 * rrow))
            nv = split(inverses[n] * 2.0)
            weights = dot(nk[0], key) + dot(nk[1], key)
            updates = dot(nv[0], value) + dot(nv[1], value)
            wu = jnp.concatenate([weights, updates], axis=1)
            scaled = split(wu * rcol)
            moved = dot_at(key, scaled[0]) + dot_at(key, scaled[1])
            step_trans = jnp.where(eye, 1.0, 0.0) - moved[:, :dk]
            step_add = moved[:, dk:]
            scores = dot_bt(query, key) * rrow
            visible = iota((tok, BLK), 1) <= REFL * iota((tok, BLK), 0) + (REFL - 1)
            scores = jnp.where(visible, scores, 0.0)
            read = dot3(split(scores), split(wu))
            project = query.astype(F32) - read[:, :dk]
            base = read[:, dk:]
            rows = slice(c * tok, (c + 1) * tok)
            if c == 0:
                trans, add = step_trans, step_add
                reach_ref[h, rows, :] = project
                base_ref[h, rows, :] = base
            else:
                before = split(jnp.concatenate([trans, add], axis=1))
                gone = dot3(split(project), before)
                reach_ref[h, rows, :] = gone[:, :dk]
                base_ref[h, rows, :] = gone[:, dk:] + base
                after = dot3(split(step_trans), before)
                trans, add = after[:, :dk], after[:, dk:] + step_add
        pair_ref[h, :, :dk] = trans
        pair_ref[h, :, dk:] = add


def chain_kernel(
    seqs, segs, heads,
    pair_ref, init_ref, reach_ref, base_ref, gain_ref, out_ref,
    rx, prefix, total, zx, outgoing, incoming,
    state_ref, put_sem, got_sem, zput_sem, zgot_sem, sput_sem, sgot_sem,
):
    dk = init_ref.shape[1]
    dv = init_ref.shape[2]
    span = seqs // heads
    me = lax.axis_index("seq")
    seg = lax.axis_index("seg")
    owner = lax.rem(me, span) == 0
    mine = me // span

    barrier = pltpu.get_barrier_semaphore()
    for d in range(1, seqs):
        pl.semaphore_signal(
            barrier, inc=1,
            device_id={"seq": lax.rem(me + d, seqs), "seg": seg}, device_id_type=MESH,
        )
    for d in range(1, segs):
        pl.semaphore_signal(
            barrier, inc=1,
            device_id={"seq": me, "seg": lax.rem(seg + d, segs)}, device_id_type=MESH,
        )
    pl.semaphore_wait(barrier, seqs + segs - 2)

    def put(h):
        return pltpu.make_async_remote_copy(
            src_ref=pair_ref.at[h], dst_ref=rx.at[me],
            send_sem=put_sem.at[h], recv_sem=got_sem.at[me],
            device_id={"seq": h * span, "seg": seg}, device_id_type=MESH,
        )

    for h in range(heads):

        @pl.when(me != h * span)
        def _():
            put(h).start()

    def zput(g):
        return pltpu.make_async_remote_copy(
            src_ref=total, dst_ref=zx.at[seg],
            send_sem=zput_sem.at[g], recv_sem=zgot_sem.at[seg],
            device_id={"seq": me, "seg": g}, device_id_type=MESH,
        )

    def zgot(g):
        return pltpu.make_async_remote_copy(
            src_ref=total, dst_ref=zx.at[g],
            send_sem=zput_sem.at[g], recv_sem=zgot_sem.at[g],
            device_id={"seq": me, "seg": g}, device_id_type=MESH,
        )

    def got(s):
        return pltpu.make_async_remote_copy(
            src_ref=rx.at[s], dst_ref=rx.at[s],
            send_sem=put_sem.at[0], recv_sem=got_sem.at[s],
            device_id={"seq": s, "seg": seg}, device_id_type=MESH,
        )

    def sput(s):
        return pltpu.make_async_remote_copy(
            src_ref=outgoing.at[s], dst_ref=incoming.at[mine],
            send_sem=sput_sem.at[s], recv_sem=sgot_sem.at[mine],
            device_id={"seq": s, "seg": seg}, device_id_type=MESH,
        )

    def sgot(h):
        return pltpu.make_async_remote_copy(
            src_ref=outgoing.at[0], dst_ref=incoming.at[h],
            send_sem=sput_sem.at[0], recv_sem=sgot_sem.at[h],
            device_id={"seq": h * span, "seg": seg}, device_id_type=MESH,
        )

    @pl.when(owner)
    def _():
        total[:, :dk] = jnp.where(iota((dk, dk), 0) == iota((dk, dk), 1), 1.0, 0.0).astype(F32)
        total[:, dk:] = jnp.zeros((dk, dv), F32)
        rx[me] = pair_ref[mine]

        def one(s, _):
            @pl.when(s != me)
            def _():
                got(s).wait_recv()

            prefix[s] = total[...]
            after = dot3(split(rx[s, :, :dk]), split(total[...]))
            total[:, :dk] = after[:, :dk]
            total[:, dk:] = after[:, dk:] + rx[s, :, dk:]
            return 0

        lax.fori_loop(0, seqs, one, 0)
        for g in range(1, segs):

            @pl.when(seg < g)
            def _():
                zput(g).start()

        state_ref[...] = init_ref[mine]
        for g in range(segs - 1):

            @pl.when(g < seg)
            def _():
                zgot(g).wait_recv()
                state_ref[...] = (
                    dot3(split(zx[g, :, :dk]), split(state_ref[...])) + zx[g, :, dk:]
                )

        def give(s, _):
            ready = dot3(split(prefix[s, :, :dk]), split(state_ref[...])) + prefix[s, :, dk:]

            @pl.when(s != me)
            def _():
                outgoing[s] = ready
                sput(s).start()

            @pl.when(s == me)
            def _():
                incoming[mine] = ready

            return 0

        lax.fori_loop(0, seqs, give, 0)

    for h in range(heads):

        @pl.when(me != h * span)
        def _():
            sgot(h).wait_recv()

        read = dot3(split(reach_ref[h]), split(incoming[h])) + base_ref[h]
        scale = lax.rsqrt(jnp.mean(read * read, axis=-1, keepdims=True) + 1e-6)
        normed = read * scale * gain_ref[h : h + 1, :]
        out_ref[:, h * dv : (h + 1) * dv] = normed.astype(BF16)

    for h in range(heads):

        @pl.when(me != h * span)
        def _():
            put(h).wait_send()

    @pl.when(owner)
    def _():
        for g in range(1, segs):

            @pl.when(seg < g)
            def _():
                zput(g).wait_send()

        def done(s, _):
            @pl.when(s != me)
            def _():
                sput(s).wait_send()

            return 0

        lax.fori_loop(0, seqs, done, 0)


def per_device(seqs, segs, query_rows, key_rows, value_rows, out_gain, initial_state):
    _, tokens, heads, dk = query_rows.shape
    dv = value_rows.shape[-1]
    steps = tokens * REFL
    query = query_rows.reshape(tokens, heads * dk)
    key = key_rows.reshape(steps, heads * dk)
    value = value_rows.reshape(steps, heads * dv)
    per = 2
    vmem = pl.BlockSpec(memory_space=pltpu.VMEM)
    count = per * (steps // BLK)
    pair, reach, base = pl.pallas_call(
        functools.partial(local_kernel, per),
        grid=(heads // per,),
        in_specs=[
            pl.BlockSpec((tokens, per * dk), lambda i: (0, i)),
            pl.BlockSpec((steps, per * dk), lambda i: (0, i)),
            pl.BlockSpec((steps, per * dv), lambda i: (0, i)),
        ],
        out_specs=[
            pl.BlockSpec((per, dk, dk + dv), lambda i: (i, 0, 0)),
            pl.BlockSpec((per, tokens, dk), lambda i: (i, 0, 0)),
            pl.BlockSpec((per, tokens, dv), lambda i: (i, 0, 0)),
        ],
        out_shape=[
            jax.ShapeDtypeStruct((heads, dk, dk + dv), F32),
            jax.ShapeDtypeStruct((heads, tokens, dk), F32),
            jax.ShapeDtypeStruct((heads, tokens, dv), F32),
        ],
        scratch_shapes=[
            pltpu.VMEM((count * SUB, BLK), F32),
            pltpu.VMEM((count * SUB, BLK), F32),
        ],
        name="local_part",
    )(query, key, value)
    wide = dk + dv
    out = pl.pallas_call(
        functools.partial(chain_kernel, seqs, segs, heads),
        in_specs=[vmem] * 5,
        out_specs=vmem,
        out_shape=jax.ShapeDtypeStruct((tokens, heads * dv), BF16),
        scratch_shapes=[
            pltpu.VMEM((seqs, dk, wide), F32),
            pltpu.VMEM((seqs, dk, wide), F32),
            pltpu.VMEM((dk, wide), F32),
            pltpu.VMEM((segs, dk, wide), F32),
            pltpu.VMEM((seqs, dk, dv), F32),
            pltpu.VMEM((heads, dk, dv), F32),
            pltpu.VMEM((dk, dv), F32),
            pltpu.SemaphoreType.DMA((heads,)),
            pltpu.SemaphoreType.DMA((seqs,)),
            pltpu.SemaphoreType.DMA((segs,)),
            pltpu.SemaphoreType.DMA((segs,)),
            pltpu.SemaphoreType.DMA((seqs,)),
            pltpu.SemaphoreType.DMA((heads,)),
        ],
        compiler_params=pltpu.CompilerParams(collective_id=0, has_side_effects=True),
        name="chain_part",
    )(pair, initial_state, reach, base, out_gain)
    return out.reshape(1, tokens, heads, dv)


def solution(mesh):
    return jax.shard_map(
        functools.partial(per_device, mesh.shape["seq"], mesh.shape["seg"]),
        mesh=mesh,
        in_specs=(
            P("seg", "seq", None, None),
            P("seg", "seq", None, None, None),
            P("seg", "seq", None, None, None),
            P(),
            P(),
        ),
        out_specs=P("seg", "seq", None, None),
        check_vma=False,
    )
```

```python
import functools

import jax
import jax.numpy as jnp
from jax import lax
from jax.experimental import pallas as pl
from jax.experimental.pallas import tpu as pltpu
from jax.sharding import PartitionSpec as P

F32 = jnp.float32
BF16 = jnp.bfloat16
REFL = 2
BLK = 128
SUB = 32
MESH = pl.DeviceIdType.MESH


def dot(a, b):
    return lax.dot_general(a, b, (((1,), (0,)), ((), ())), preferred_element_type=F32)


def dot_bt(a, b):
    return lax.dot_general(a, b, (((1,), (1,)), ((), ())), preferred_element_type=F32)


def dot_at(a, b):
    return lax.dot_general(a, b, (((0,), (0,)), ((), ())), preferred_element_type=F32)


def split(x):
    high = x.astype(BF16)
    return high, (x - high.astype(F32)).astype(BF16)


def dot3(a, b):
    ah, al = a
    bh, bl = b
    return dot(jnp.concatenate([ah, al], 1), jnp.concatenate([bh, bh], 0)) + dot(ah, bl)


def dot2(a, exact):
    return dot(jnp.concatenate(a, 1), jnp.concatenate([exact, exact], 0))


def iota(shape, axis):
    return lax.broadcasted_iota(jnp.int32, shape, axis)


def grouped(x, size, odd):
    return [x[g * size : (g + 1) * size] for g in range(odd, x.shape[0] // size, 2)]


def factors(first, per, heads, nblk, kf, vf, dsc, nsc, kb, scaled_hi, scaled_lo, before, pair):
    dk = kf.shape[1]
    row, col = iota((BLK, BLK), 0), iota((BLK, BLK), 1)
    eye = row == col
    lane = iota((SUB, BLK), 1)
    count = per * nblk

    keys, lowers, rcols, rrows = [], [], [], []
    for n in range(count):
        h, c = n // nblk, n % nblk
        key = kf[pl.ds(c * BLK * heads + first + h, BLK, stride=heads), :].astype(BF16)
        kb[first + h, c] = key
        gram = dot_bt(key, key)
        diag = jnp.where(eye, gram, 0.0)
        rcol = lax.rsqrt(jnp.sum(diag, axis=1, keepdims=True) + 1e-6)
        rrow = lax.rsqrt(jnp.sum(diag, axis=0, keepdims=True) + 1e-6)
        lower = jnp.where(row > col, gram * (2.0 * rcol) * rrow, 0.0)
        packed = lower[:SUB]
        for g in range(1, BLK // SUB):
            packed = jnp.where(lane // SUB == g, lower[g * SUB : (g + 1) * SUB], packed)
        dsc[n * SUB : (n + 1) * SUB, :] = packed
        keys.append(key)
        lowers.append(lower)
        rcols.append(rcol)
        rrows.append(rrow)

    lane_c = iota((count, BLK), 1)
    solved = []
    for i in range(SUB):
        line = dsc[pl.ds(i, count, stride=SUB), :]
        total = jnp.where(lane_c % SUB == i, 1.0, 0.0)
        for j in range(i):
            factor = jnp.take_along_axis(line, (lane_c // SUB) * SUB + j, axis=1)
            total = total - factor * solved[j]
        solved.append(total)
        nsc[pl.ds(i, count, stride=SUB), :] = total

    inverses = []
    for n in range(count):
        packed = nsc[n * SUB : (n + 1) * SUB, :]
        inverses.append(
            jnp.concatenate(
                [jnp.where(lane // SUB == g, packed, 0.0) for g in range(BLK // SUB)], axis=0
            )
        )
    half = BLK // 2
    size = SUB
    while size < BLK:
        paired = iota((half, BLK), 1) // size == 2 * (iota((half, BLK), 0) // size)
        for n in range(count):
            inv = split(inverses[n])
            odd = jnp.concatenate(grouped(lowers[n], size, 1), 0)
            part = dot3(split(jnp.where(paired, odd, 0.0)), inv)
            blank = jnp.zeros((size, BLK), F32)
            spread = []
            for g in range(half // size):
                spread += [blank, part[g * size : (g + 1) * size]]
            own = tuple(jnp.concatenate(grouped(x, size, 1), 0) for x in inv)
            fill = dot3(own, split(jnp.concatenate(spread, 0)))
            even, odd = grouped(inverses[n], size, 0), grouped(inverses[n], size, 1)
            rows = []
            for g in range(half // size):
                rows += [even[g], odd[g] - fill[g * size : (g + 1) * size]]
            inverses[n] = jnp.concatenate(rows, 0)
        size *= 2

    for h in range(per):
        trans = add = None
        for c in range(nblk):
            n = h * nblk + c
            key, rcol, rrow = keys[n], rcols[n], rrows[n]
            value = vf[pl.ds(c * BLK * heads + first + h, BLK, stride=heads), :].astype(BF16)
            weights = dot2(split(inverses[n] * (2.0 * rrow)), key)
            updates = dot2(split(inverses[n] * 2.0), value)
            scaled = split(jnp.concatenate([weights, updates], axis=1) * rcol)
            scaled_hi[first + h, c] = scaled[0]
            scaled_lo[first + h, c] = scaled[1]
            moved = dot_at(jnp.concatenate([key, key], 0), jnp.concatenate(scaled, 0))
            step_trans = jnp.where(eye, 1.0, 0.0) - moved[:, :dk]
            step_add = moved[:, dk:]
            if c == 0:
                trans, add = step_trans, step_add
            else:
                so_far = jnp.concatenate([trans, add], axis=1)
                before[first + h, c] = so_far
                after = dot3(split(step_trans), split(so_far))
                trans, add = after[:, :dk], after[:, dk:] + step_add
        pair[first + h, :, :dk] = trans
        pair[first + h, :, dk:] = add


def readers(h, heads, nblk, qf, kb, scaled_hi, scaled_lo, before, reach, base):
    dk = qf.shape[1]
    tok = BLK // REFL
    visible = iota((tok, BLK), 1) <= REFL * iota((tok, BLK), 0) + (REFL - 1)
    for c in range(nblk):
        query = qf[pl.ds(c * tok * heads + h, tok, stride=heads), :]
        scores = jnp.where(visible, dot_bt(query.astype(BF16), kb[h, c]), 0.0)
        read = dot3(split(scores), (scaled_hi[h, c], scaled_lo[h, c]))
        project = query - read[:, :dk]
        local = read[:, dk:]
        rows = slice(c * tok, (c + 1) * tok)
        if c == 0:
            reach[h, rows, :] = project
            base[h, rows, :] = local
        else:
            gone = dot3(split(project), split(before[h, c]))
            reach[h, rows, :] = gone[:, :dk]
            base[h, rows, :] = gone[:, dk:] + local


def kernel(
    seqs, segs, heads, per,
    q_ref, k_ref, v_ref, gain_ref, init_ref, out_ref,
    qf, kf, vf, dsc, nsc, kb, scaled_hi, scaled_lo, before, pair, reach, base,
    rx, prefix, own_prefix, total, zx, first_state, zstate, own_state, state,
    put_sem, got_sem, zput_sem, zgot_sem, pput_sem, pgot_sem, sput_sem, sgot_sem,
):
    dk = init_ref.shape[1]
    dv = init_ref.shape[2]
    nblk = k_ref.shape[0] // (heads * BLK)
    span = seqs // heads
    me = lax.axis_index("seq")
    seg = lax.axis_index("seg")
    owner = lax.rem(me, span) == 0
    mine = me // span

    barrier = pltpu.get_barrier_semaphore()
    for d in range(1, seqs):
        pl.semaphore_signal(
            barrier, inc=1,
            device_id={"seq": lax.rem(me + d, seqs), "seg": seg}, device_id_type=MESH,
        )
    for d in range(1, segs):
        pl.semaphore_signal(
            barrier, inc=1,
            device_id={"seq": me, "seg": lax.rem(seg + d, segs)}, device_id_type=MESH,
        )

    def copy(src, dst, put, got, to_seq, to_seg):
        return pltpu.make_async_remote_copy(
            src_ref=src, dst_ref=dst, send_sem=put, recv_sem=got,
            device_id={"seq": to_seq, "seg": to_seg}, device_id_type=MESH,
        )

    def put(h):
        return copy(pair.at[h], rx.at[me], put_sem.at[h], got_sem.at[me], h * span, seg)

    def got(s):
        return copy(rx.at[s], rx.at[s], put_sem.at[0], got_sem.at[s], s, seg)

    def pput(s):
        return copy(prefix.at[s], own_prefix.at[mine], pput_sem.at[s], pgot_sem.at[mine], s, seg)

    def pgot(h):
        return copy(prefix.at[0], own_prefix.at[h], pput_sem.at[0], pgot_sem.at[h], h * span, seg)

    def sput(s):
        return copy(state, own_state.at[mine], sput_sem.at[s], sgot_sem.at[mine], s, seg)

    def sgot(h):
        return copy(state, own_state.at[h], sput_sem.at[0], sgot_sem.at[h], h * span, seg)

    def zput(g):
        return copy(total, zx.at[seg], zput_sem.at[g], zgot_sem.at[seg], me, g)

    def zgot(g):
        return copy(total, zx.at[g], zput_sem.at[g], zgot_sem.at[g], me, g)

    def fput(g):
        return copy(first_state, zstate, zput_sem.at[g], zgot_sem.at[0], me, g)

    kf[...] = k_ref[...].astype(F32)
    vf[...] = v_ref[...].astype(F32)
    qf[...] = q_ref[...].astype(F32)

    def local(i, _):
        factors(i * per, per, heads, nblk, kf, vf, dsc, nsc, kb, scaled_hi, scaled_lo, before, pair)

        @pl.when(i == 0)
        def _():
            pl.semaphore_wait(barrier, seqs + segs - 2)

        for d in range(per):
            h = i * per + d

            @pl.when(me != h * span)
            def _():
                put(h).start()

        return 0

    lax.fori_loop(0, heads // per, local, 0)

    def reading(h, _):
        readers(h, heads, nblk, qf, kb, scaled_hi, scaled_lo, before, reach, base)
        return 0

    lax.fori_loop(0, heads, reading, 0)

    @pl.when(owner)
    def _():
        total[:, :dk] = jnp.where(iota((dk, dk), 0) == iota((dk, dk), 1), 1.0, 0.0).astype(F32)
        total[:, dk:] = jnp.zeros((dk, dv), F32)
        rx[me] = pair[mine]

        def one(s, _):
            @pl.when(s != me)
            def _():
                got(s).wait_recv()

            so_far = total[...]
            prefix[s] = so_far

            @pl.when(s != me)
            def _():
                pput(s).start()

            @pl.when(s == me)
            def _():
                own_prefix[mine] = so_far

            after = dot3(split(rx[s, :, :dk]), split(so_far))
            total[:, :dk] = after[:, :dk]
            total[:, dk:] = after[:, dk:] + rx[s, :, dk:]
            return 0

        lax.fori_loop(0, seqs, one, 0)

        @pl.when(seg == 0)
        def _():
            first_state[...] = dot3(split(total[:, :dk]), split(init_ref[mine])) + total[:, dk:]
            for g in range(1, segs):
                fput(g).start()

        for g in range(2, segs):

            @pl.when((seg > 0) & (seg < g))
            def _():
                zput(g).start()

    def joining(h, _):
        @pl.when(me != h * span)
        def _():
            pgot(h).wait_recv()

        gone = dot3(split(reach[h]), split(own_prefix[h]))
        reach[h] = gone[:, :dk]
        base[h] = gone[:, dk:] + base[h]
        return 0

    lax.fori_loop(0, heads, joining, 0)

    @pl.when(owner)
    def _():
        @pl.when(seg == 0)
        def _():
            state[...] = init_ref[mine]

        @pl.when(seg > 0)
        def _():
            fput(0).wait_recv()
            state[...] = zstate[...]

        for g in range(1, segs - 1):

            @pl.when(g < seg)
            def _():
                zgot(g).wait_recv()
                state[...] = dot3(split(zx[g, :, :dk]), split(state[...])) + zx[g, :, dk:]

        def give(s, _):
            @pl.when(s != me)
            def _():
                sput(s).start()

            return 0

        lax.fori_loop(0, seqs, give, 0)
        own_state[mine] = state[...]

    for h in range(heads):

        @pl.when(me != h * span)
        def _():
            sgot(h).wait_recv()

        read = dot3(split(reach[h]), split(own_state[h])) + base[h]
        scale = lax.rsqrt(jnp.mean(read * read, axis=-1, keepdims=True) + 1e-6)
        normed = read * scale * gain_ref[h : h + 1, :]
        qf[pl.ds(h, read.shape[0], stride=heads), :] = normed
    out_ref[...] = qf[...].astype(BF16)

    for h in range(heads):

        @pl.when(me != h * span)
        def _():
            put(h).wait_send()

    @pl.when(owner)
    def _():
        @pl.when(seg == 0)
        def _():
            for g in range(1, segs):
                fput(g).wait_send()

        for g in range(2, segs):

            @pl.when((seg > 0) & (seg < g))
            def _():
                zput(g).wait_send()

        def done(s, _):
            @pl.when(s != me)
            def _():
                pput(s).wait_send()
                sput(s).wait_send()

            return 0

        lax.fori_loop(0, seqs, done, 0)


def per_device(seqs, segs, query_rows, key_rows, value_rows, out_gain, initial_state):
    _, tokens, heads, dk = query_rows.shape
    dv = value_rows.shape[-1]
    steps = tokens * REFL
    nblk = steps // BLK
    per = 2
    count = per * nblk
    wide = dk + dv
    vmem = pl.BlockSpec(memory_space=pltpu.VMEM)
    dma = pltpu.SemaphoreType.DMA
    out = pl.pallas_call(
        functools.partial(kernel, seqs, segs, heads, per),
        in_specs=[vmem] * 5,
        out_specs=vmem,
        out_shape=jax.ShapeDtypeStruct((tokens * heads, dv), BF16),
        scratch_shapes=[
            pltpu.VMEM((tokens * heads, dk), F32),
            pltpu.VMEM((steps * heads, dk), F32),
            pltpu.VMEM((steps * heads, dv), F32),
            pltpu.VMEM((count * SUB, BLK), F32),
            pltpu.VMEM((count * SUB, BLK), F32),
            pltpu.VMEM((heads, nblk, BLK, dk), BF16),
            pltpu.VMEM((heads, nblk, BLK, wide), BF16),
            pltpu.VMEM((heads, nblk, BLK, wide), BF16),
            pltpu.VMEM((heads, nblk, dk, wide), F32),
            pltpu.VMEM((heads, dk, wide), F32),
            pltpu.VMEM((heads, tokens, dk), F32),
            pltpu.VMEM((heads, tokens, dv), F32),
            pltpu.VMEM((seqs, dk, wide), F32),
            pltpu.VMEM((seqs, dk, wide), F32),
            pltpu.VMEM((heads, dk, wide), F32),
            pltpu.VMEM((dk, wide), F32),
            pltpu.VMEM((segs, dk, wide), F32),
            pltpu.VMEM((dk, dv), F32),
            pltpu.VMEM((dk, dv), F32),
            pltpu.VMEM((heads, dk, dv), F32),
            pltpu.VMEM((dk, dv), F32),
            dma((heads,)),
            dma((seqs,)),
            dma((segs,)),
            dma((segs,)),
            dma((seqs,)),
            dma((heads,)),
            dma((seqs,)),
            dma((heads,)),
        ],
        compiler_params=pltpu.CompilerParams(collective_id=0, has_side_effects=True),
        name="delta_product",
    )(
        query_rows.reshape(tokens * heads, dk),
        key_rows.reshape(steps * heads, dk),
        value_rows.reshape(steps * heads, dv),
        out_gain,
        initial_state,
    )
    return out.reshape(1, tokens, heads, dv)


def solution(mesh):
    return jax.shard_map(
        functools.partial(per_device, mesh.shape["seq"], mesh.shape["seg"]),
        mesh=mesh,
        in_specs=(
            P("seg", "seq", None, None),
            P("seg", "seq", None, None, None),
            P("seg", "seq", None, None, None),
            P(),
            P(),
        ),
        out_specs=P("seg", "seq", None, None),
        check_vma=False,
    )
```

```python
import functools

import jax
import jax.numpy as jnp
from jax import lax
from jax.experimental import pallas as pl
from jax.experimental.pallas import tpu as pltpu
from jax.sharding import PartitionSpec as P

F32 = jnp.float32
BF16 = jnp.bfloat16
REFL = 2
BLK = 128
SUB = 16
MESH = pl.DeviceIdType.MESH


def dot(a, b):
    return lax.dot_general(a, b, (((1,), (0,)), ((), ())), preferred_element_type=F32)


def dot_bt(a, b):
    return lax.dot_general(a, b, (((1,), (1,)), ((), ())), preferred_element_type=F32)


def dot_at(a, b):
    return lax.dot_general(a, b, (((0,), (0,)), ((), ())), preferred_element_type=F32)


def split(x):
    high = x.astype(BF16)
    return high, (x - high.astype(F32)).astype(BF16)


def dot3(a, b):
    ah, al = a
    bh, bl = b
    return dot(jnp.concatenate([ah, al], 1), jnp.concatenate([bh, bh], 0)) + dot(ah, bl)


def dot2(a, exact):
    return dot(jnp.concatenate(a, 1), jnp.concatenate([exact, exact], 0))


def iota(shape, axis):
    return lax.broadcasted_iota(jnp.int32, shape, axis)


def grouped(x, size, odd):
    return [x[g * size : (g + 1) * size] for g in range(odd, x.shape[0] // size, 2)]


def factors(first, per, heads, nblk, kf, vf, dsc, nsc, kb, scaled_hi, scaled_lo, before, pair):
    dk = kf.shape[1]
    row, col = iota((BLK, BLK), 0), iota((BLK, BLK), 1)
    eye = row == col
    lane = iota((SUB, BLK), 1)
    count = per * nblk

    keys, lowers, rcols, rrows = [], [], [], []
    for n in range(count):
        h, c = n // nblk, n % nblk
        key = kf[pl.ds(c * BLK * heads + first + h, BLK, stride=heads), :].astype(BF16)
        kb[first + h, c] = key
        gram = dot_bt(key, key)
        diag = jnp.where(eye, gram, 0.0)
        rcol = lax.rsqrt(jnp.sum(diag, axis=1, keepdims=True) + 1e-6)
        rrow = lax.rsqrt(jnp.sum(diag, axis=0, keepdims=True) + 1e-6)
        lower = jnp.where(row > col, gram * (2.0 * rcol) * rrow, 0.0)
        packed = lower[:SUB]
        for g in range(1, BLK // SUB):
            packed = jnp.where(lane // SUB == g, lower[g * SUB : (g + 1) * SUB], packed)
        dsc[n * SUB : (n + 1) * SUB, :] = packed
        keys.append(key)
        lowers.append(lower)
        rcols.append(rcol)
        rrows.append(rrow)

    lane_c = iota((count, BLK), 1)
    solved = []
    for i in range(SUB):
        line = dsc[pl.ds(i, count, stride=SUB), :]
        total = jnp.where(lane_c % SUB == i, 1.0, 0.0)
        for j in range(i):
            factor = jnp.take_along_axis(line, (lane_c // SUB) * SUB + j, axis=1)
            total = total - factor * solved[j]
        solved.append(total)
        nsc[pl.ds(i, count, stride=SUB), :] = total

    inverses = []
    for n in range(count):
        packed = nsc[n * SUB : (n + 1) * SUB, :]
        inverses.append(
            jnp.concatenate(
                [jnp.where(lane // SUB == g, packed, 0.0) for g in range(BLK // SUB)], axis=0
            )
        )
    half = BLK // 2
    size = SUB
    while size < BLK:
        paired = iota((half, BLK), 1) // size == 2 * (iota((half, BLK), 0) // size)
        for n in range(count):
            inv = split(inverses[n])
            odd = jnp.concatenate(grouped(lowers[n], size, 1), 0)
            part = dot3(split(jnp.where(paired, odd, 0.0)), inv)
            blank = jnp.zeros((size, BLK), F32)
            spread = []
            for g in range(half // size):
                spread += [blank, part[g * size : (g + 1) * size]]
            own = tuple(jnp.concatenate(grouped(x, size, 1), 0) for x in inv)
            fill = dot3(own, split(jnp.concatenate(spread, 0)))
            even, odd = grouped(inverses[n], size, 0), grouped(inverses[n], size, 1)
            rows = []
            for g in range(half // size):
                rows += [even[g], odd[g] - fill[g * size : (g + 1) * size]]
            inverses[n] = jnp.concatenate(rows, 0)
        size *= 2

    for h in range(per):
        trans = add = None
        for c in range(nblk):
            n = h * nblk + c
            key, rcol, rrow = keys[n], rcols[n], rrows[n]
            value = vf[pl.ds(c * BLK * heads + first + h, BLK, stride=heads), :].astype(BF16)
            weights = dot2(split(inverses[n] * (2.0 * rrow)), key)
            updates = dot2(split(inverses[n] * 2.0), value)
            scaled = split(jnp.concatenate([weights, updates], axis=1) * rcol)
            scaled_hi[first + h, c] = scaled[0]
            scaled_lo[first + h, c] = scaled[1]
            moved = dot_at(jnp.concatenate([key, key], 0), jnp.concatenate(scaled, 0))
            step_trans = jnp.where(eye, 1.0, 0.0) - moved[:, :dk]
            step_add = moved[:, dk:]
            if c == 0:
                trans, add = step_trans, step_add
            else:
                so_far = jnp.concatenate([trans, add], axis=1)
                before[first + h, c] = so_far
                after = dot3(split(step_trans), split(so_far))
                trans, add = after[:, :dk], after[:, dk:] + step_add
        pair[first + h, :, :dk] = trans
        pair[first + h, :, dk:] = add


def readers(h, heads, nblk, qf, kb, scaled_hi, scaled_lo, before, reach, base):
    dk = qf.shape[1]
    tok = BLK // REFL
    visible = iota((tok, BLK), 1) <= REFL * iota((tok, BLK), 0) + (REFL - 1)
    for c in range(nblk):
        query = qf[pl.ds(c * tok * heads + h, tok, stride=heads), :]
        scores = jnp.where(visible, dot_bt(query.astype(BF16), kb[h, c]), 0.0)
        read = dot3(split(scores), (scaled_hi[h, c], scaled_lo[h, c]))
        project = query - read[:, :dk]
        local = read[:, dk:]
        rows = slice(c * tok, (c + 1) * tok)
        if c == 0:
            reach[h, rows, :] = project
            base[h, rows, :] = local
        else:
            gone = dot3(split(project), split(before[h, c]))
            reach[h, rows, :] = gone[:, :dk]
            base[h, rows, :] = gone[:, dk:] + local


def kernel(
    seqs, segs, heads, per,
    q_ref, k_ref, v_ref, gain_ref, init_ref, out_ref,
    qf, kf, vf, dsc, nsc, kb, scaled_hi, scaled_lo, before, pair, reach, base,
    rx, prefix, outgoing, total, zx, first_state, zstate, own_state, state,
    put_sem, got_sem, zput_sem, zgot_sem, sput_sem, sgot_sem,
):
    dk = init_ref.shape[1]
    dv = init_ref.shape[2]
    nblk = k_ref.shape[0] // (heads * BLK)
    span = seqs // heads
    me = lax.axis_index("seq")
    seg = lax.axis_index("seg")
    owner = lax.rem(me, span) == 0
    mine = me // span

    barrier = pltpu.get_barrier_semaphore()
    for d in range(1, seqs):
        pl.semaphore_signal(
            barrier, inc=1,
            device_id={"seq": lax.rem(me + d, seqs), "seg": seg}, device_id_type=MESH,
        )
    for d in range(1, segs):
        pl.semaphore_signal(
            barrier, inc=1,
            device_id={"seq": me, "seg": lax.rem(seg + d, segs)}, device_id_type=MESH,
        )

    def copy(src, dst, put, got, to_seq, to_seg):
        return pltpu.make_async_remote_copy(
            src_ref=src, dst_ref=dst, send_sem=put, recv_sem=got,
            device_id={"seq": to_seq, "seg": to_seg}, device_id_type=MESH,
        )

    def put(h):
        return copy(pair.at[h], rx.at[me], put_sem.at[h], got_sem.at[me], h * span, seg)

    def got(s):
        return copy(rx.at[s], rx.at[s], put_sem.at[0], got_sem.at[s], s, seg)

    def sput(s):
        return copy(outgoing.at[s], own_state.at[mine], sput_sem.at[s], sgot_sem.at[mine], s, seg)

    def sgot(h):
        return copy(outgoing.at[0], own_state.at[h], sput_sem.at[0], sgot_sem.at[h], h * span, seg)

    def zput(g):
        return copy(total, zx.at[seg], zput_sem.at[g], zgot_sem.at[seg], me, g)

    def zgot(g):
        return copy(total, zx.at[g], zput_sem.at[g], zgot_sem.at[g], me, g)

    def fput(g):
        return copy(first_state, zstate, zput_sem.at[g], zgot_sem.at[0], me, g)

    kf[...] = k_ref[...].astype(F32)
    vf[...] = v_ref[...].astype(F32)
    qf[...] = q_ref[...].astype(F32)

    def local(i, _):
        turn = lax.rem(i + 1 + mine // per, heads // per)
        factors(turn * per, per, heads, nblk, kf, vf, dsc, nsc, kb, scaled_hi, scaled_lo, before, pair)

        @pl.when(i == 0)
        def _():
            pl.semaphore_wait(barrier, seqs + segs - 2)

        for d in range(per):
            h = turn * per + d

            @pl.when(me != h * span)
            def _():
                put(h).start()

        return 0

    lax.fori_loop(0, heads // per, local, 0)

    def reading(h, _):
        readers(h, heads, nblk, qf, kb, scaled_hi, scaled_lo, before, reach, base)
        return 0

    lax.fori_loop(0, heads, reading, 0)

    @pl.when(owner)
    def _():
        total[:, :dk] = jnp.where(iota((dk, dk), 0) == iota((dk, dk), 1), 1.0, 0.0).astype(F32)
        total[:, dk:] = jnp.zeros((dk, dv), F32)
        rx[me] = pair[mine]

        def one(s, _):
            @pl.when(s != me)
            def _():
                got(s).wait_recv()

            so_far = total[...]
            prefix[s] = so_far
            after = dot3(split(rx[s, :, :dk]), split(so_far))
            total[:, :dk] = after[:, :dk]
            total[:, dk:] = after[:, dk:] + rx[s, :, dk:]
            return 0

        lax.fori_loop(0, seqs, one, 0)

        @pl.when(seg == 0)
        def _():
            first_state[...] = dot3(split(total[:, :dk]), split(init_ref[mine])) + total[:, dk:]
            for g in range(1, segs):
                fput(g).start()

        for g in range(2, segs):

            @pl.when((seg > 0) & (seg < g))
            def _():
                zput(g).start()

    @pl.when(owner)
    def _():
        @pl.when(seg == 0)
        def _():
            state[...] = init_ref[mine]

        @pl.when(seg > 0)
        def _():
            fput(0).wait_recv()
            state[...] = zstate[...]

        for g in range(1, segs - 1):

            @pl.when(g < seg)
            def _():
                zgot(g).wait_recv()
                state[...] = dot3(split(zx[g, :, :dk]), split(state[...])) + zx[g, :, dk:]

        def give(s, _):
            ready = dot3(split(prefix[s, :, :dk]), split(state[...])) + prefix[s, :, dk:]

            @pl.when(s != me)
            def _():
                outgoing[s] = ready
                sput(s).start()

            @pl.when(s == me)
            def _():
                own_state[mine] = ready

            return 0

        lax.fori_loop(0, seqs, give, 0)

    for h in range(heads):

        @pl.when(me != h * span)
        def _():
            sgot(h).wait_recv()

        read = dot3(split(reach[h]), split(own_state[h])) + base[h]
        scale = lax.rsqrt(jnp.mean(read * read, axis=-1, keepdims=True) + 1e-6)
        normed = read * scale * gain_ref[h : h + 1, :]
        qf[pl.ds(h, read.shape[0], stride=heads), :] = normed
    out_ref[...] = qf[...].astype(BF16)

    for h in range(heads):

        @pl.when(me != h * span)
        def _():
            put(h).wait_send()

    @pl.when(owner)
    def _():
        @pl.when(seg == 0)
        def _():
            for g in range(1, segs):
                fput(g).wait_send()

        for g in range(2, segs):

            @pl.when((seg > 0) & (seg < g))
            def _():
                zput(g).wait_send()

        def done(s, _):
            @pl.when(s != me)
            def _():
                sput(s).wait_send()

            return 0

        lax.fori_loop(0, seqs, done, 0)


def per_device(seqs, segs, query_rows, key_rows, value_rows, out_gain, initial_state):
    _, tokens, heads, dk = query_rows.shape
    dv = value_rows.shape[-1]
    steps = tokens * REFL
    nblk = steps // BLK
    per = 2
    count = per * nblk
    wide = dk + dv
    vmem = pl.BlockSpec(memory_space=pltpu.VMEM)
    dma = pltpu.SemaphoreType.DMA
    out = pl.pallas_call(
        functools.partial(kernel, seqs, segs, heads, per),
        in_specs=[vmem] * 5,
        out_specs=vmem,
        out_shape=jax.ShapeDtypeStruct((tokens * heads, dv), BF16),
        scratch_shapes=[
            pltpu.VMEM((tokens * heads, dk), F32),
            pltpu.VMEM((steps * heads, dk), F32),
            pltpu.VMEM((steps * heads, dv), F32),
            pltpu.VMEM((count * SUB, BLK), F32),
            pltpu.VMEM((count * SUB, BLK), F32),
            pltpu.VMEM((heads, nblk, BLK, dk), BF16),
            pltpu.VMEM((heads, nblk, BLK, wide), BF16),
            pltpu.VMEM((heads, nblk, BLK, wide), BF16),
            pltpu.VMEM((heads, nblk, dk, wide), F32),
            pltpu.VMEM((heads, dk, wide), F32),
            pltpu.VMEM((heads, tokens, dk), F32),
            pltpu.VMEM((heads, tokens, dv), F32),
            pltpu.VMEM((seqs, dk, wide), F32),
            pltpu.VMEM((seqs, dk, wide), F32),
            pltpu.VMEM((seqs, dk, dv), F32),
            pltpu.VMEM((dk, wide), F32),
            pltpu.VMEM((segs, dk, wide), F32),
            pltpu.VMEM((dk, dv), F32),
            pltpu.VMEM((dk, dv), F32),
            pltpu.VMEM((heads, dk, dv), F32),
            pltpu.VMEM((dk, dv), F32),
            dma((heads,)),
            dma((seqs,)),
            dma((segs,)),
            dma((segs,)),
            dma((seqs,)),
            dma((heads,)),
        ],
        compiler_params=pltpu.CompilerParams(collective_id=0, has_side_effects=True),
        name="delta_product",
    )(
        query_rows.reshape(tokens * heads, dk),
        key_rows.reshape(steps * heads, dk),
        value_rows.reshape(steps * heads, dv),
        out_gain,
        initial_state,
    )
    return out.reshape(1, tokens, heads, dv)


def solution(mesh):
    return jax.shard_map(
        functools.partial(per_device, mesh.shape["seq"], mesh.shape["seg"]),
        mesh=mesh,
        in_specs=(
            P("seg", "seq", None, None),
            P("seg", "seq", None, None, None),
            P("seg", "seq", None, None, None),
            P(),
            P(),
        ),
        out_specs=P("seg", "seq", None, None),
        check_vma=False,
    )
```

```python
import functools

import jax
import jax.numpy as jnp
from jax import lax
from jax.experimental import pallas as pl
from jax.experimental.pallas import tpu as pltpu
from jax.sharding import PartitionSpec as P

F32 = jnp.float32
BF16 = jnp.bfloat16
REFL = 2
BLK = 128
SUB = 16
LANES = 128
MESH = pl.DeviceIdType.MESH


def dot(a, b):
    return lax.dot_general(a, b, (((1,), (0,)), ((), ())), preferred_element_type=F32)


def dot_bt(a, b):
    return lax.dot_general(a, b, (((1,), (1,)), ((), ())), preferred_element_type=F32)


def dot_at(a, b):
    return lax.dot_general(a, b, (((0,), (0,)), ((), ())), preferred_element_type=F32)


def split(x):
    high = x.astype(BF16)
    return high, (x - high.astype(F32)).astype(BF16)


def dot3(a, b):
    ah, al = a
    bh, bl = b
    rows, width = ah.shape[0], bh.shape[1]
    both = jnp.concatenate([ah, al], 0)
    if width <= LANES:
        full = dot(both, jnp.concatenate([bh, bl], 1))
        return full[:rows, :width] + (full[:rows, width:] + full[rows:, :width])
    full = dot(both, bh)
    return full[:rows] + (full[rows:] + dot(ah, bl))


def dot2(a, exact):
    rows = a[0].shape[0]
    full = dot(jnp.concatenate(a, 0), exact)
    return full[:rows] + full[rows:]


def iota(shape, axis):
    return lax.broadcasted_iota(jnp.int32, shape, axis)


def grouped(x, size, odd):
    return [x[g * size : (g + 1) * size] for g in range(odd, x.shape[0] // size, 2)]


def factors(first, per, heads, nblk, kf, vf, dsc, nsc, kb, scaled_hi, scaled_lo, before, pair):
    dk = kf.shape[1]
    row, col = iota((BLK, BLK), 0), iota((BLK, BLK), 1)
    eye = row == col
    lane = iota((SUB, BLK), 1)
    count = per * nblk

    keys, lowers, rcols, rrows = [], [], [], []
    for n in range(count):
        h, c = n // nblk, n % nblk
        key = kf[pl.ds(c * BLK * heads + first + h, BLK, stride=heads), :].astype(BF16)
        kb[first + h, c] = key
        gram = dot_bt(key, key)
        diag = jnp.where(eye, gram, 0.0)
        rcol = lax.rsqrt(jnp.sum(diag, axis=1, keepdims=True) + 1e-6)
        rrow = lax.rsqrt(jnp.sum(diag, axis=0, keepdims=True) + 1e-6)
        lower = jnp.where(row > col, gram * (2.0 * rcol) * rrow, 0.0)
        packed = lower[:SUB]
        for g in range(1, BLK // SUB):
            packed = jnp.where(lane // SUB == g, lower[g * SUB : (g + 1) * SUB], packed)
        dsc[n * SUB : (n + 1) * SUB, :] = packed
        keys.append(key)
        lowers.append(lower)
        rcols.append(rcol)
        rrows.append(rrow)

    lane_c = iota((count, BLK), 1)
    solved = []
    for i in range(SUB):
        line = dsc[pl.ds(i, count, stride=SUB), :]
        total = jnp.where(lane_c % SUB == i, 1.0, 0.0)
        for j in range(i):
            factor = jnp.take_along_axis(line, (lane_c // SUB) * SUB + j, axis=1)
            total = total - factor * solved[j]
        solved.append(total)
        nsc[pl.ds(i, count, stride=SUB), :] = total

    inverses = []
    for n in range(count):
        packed = nsc[n * SUB : (n + 1) * SUB, :]
        inverses.append(
            jnp.concatenate(
                [jnp.where(lane // SUB == g, packed, 0.0) for g in range(BLK // SUB)], axis=0
            )
        )
    half = BLK // 2
    size = SUB
    while size < BLK:
        paired = iota((half, BLK), 1) // size == 2 * (iota((half, BLK), 0) // size)
        for n in range(count):
            inv = split(inverses[n])
            odd = jnp.concatenate(grouped(lowers[n], size, 1), 0)
            part = dot3(split(jnp.where(paired, odd, 0.0)), inv)
            blank = jnp.zeros((size, BLK), F32)
            spread = []
            for g in range(half // size):
                spread += [blank, part[g * size : (g + 1) * size]]
            own = tuple(jnp.concatenate(grouped(x, size, 1), 0) for x in inv)
            fill = dot3(own, split(jnp.concatenate(spread, 0)))
            even, odd = grouped(inverses[n], size, 0), grouped(inverses[n], size, 1)
            rows = []
            for g in range(half // size):
                rows += [even[g], odd[g] - fill[g * size : (g + 1) * size]]
            inverses[n] = jnp.concatenate(rows, 0)
        size *= 2

    for h in range(per):
        trans = add = None
        for c in range(nblk):
            n = h * nblk + c
            key, rcol, rrow = keys[n], rcols[n], rrows[n]
            value = vf[pl.ds(c * BLK * heads + first + h, BLK, stride=heads), :].astype(BF16)
            weights = dot2(split(inverses[n] * (2.0 * rrow)), key)
            updates = dot2(split(inverses[n] * 2.0), value)
            scaled = split(jnp.concatenate([weights, updates], axis=1) * rcol)
            scaled_hi[first + h, c] = scaled[0]
            scaled_lo[first + h, c] = scaled[1]
            moved = dot_at(key, scaled[0]) + dot_at(key, scaled[1])
            step_trans = jnp.where(eye, 1.0, 0.0) - moved[:, :dk]
            step_add = moved[:, dk:]
            if c == 0:
                trans, add = step_trans, step_add
            else:
                so_far = jnp.concatenate([trans, add], axis=1)
                before[first + h, c] = so_far
                after = dot3(split(step_trans), split(so_far))
                trans, add = after[:, :dk], after[:, dk:] + step_add
        pair[first + h, :, :dk] = trans
        pair[first + h, :, dk:] = add


def readers(h, heads, nblk, qf, kb, scaled_hi, scaled_lo, before, reach, base):
    dk = qf.shape[1]
    tok = BLK // REFL
    visible = iota((tok, BLK), 1) <= REFL * iota((tok, BLK), 0) + (REFL - 1)
    for c in range(nblk):
        query = qf[pl.ds(c * tok * heads + h, tok, stride=heads), :]
        scores = jnp.where(visible, dot_bt(query.astype(BF16), kb[h, c]), 0.0)
        read = dot3(split(scores), (scaled_hi[h, c], scaled_lo[h, c]))
        project = query - read[:, :dk]
        local = read[:, dk:]
        rows = slice(c * tok, (c + 1) * tok)
        if c == 0:
            reach[h, rows, :] = project
            base[h, rows, :] = local
        else:
            gone = dot3(split(project), split(before[h, c]))
            reach[h, rows, :] = gone[:, :dk]
            base[h, rows, :] = gone[:, dk:] + local


def kernel(
    seqs, segs, heads, per,
    q_ref, k_ref, v_ref, gain_ref, init_ref, out_ref,
    qf, kf, vf, dsc, nsc, kb, scaled_hi, scaled_lo, before, pair, reach, base,
    rx, prefix, outgoing, total, tree, zx, first_state, zstate, own_state, state,
    put_sem, got_sem, zput_sem, zgot_sem, sput_sem, sgot_sem,
):
    dk = init_ref.shape[1]
    dv = init_ref.shape[2]
    nblk = k_ref.shape[0] // (heads * BLK)
    span = seqs // heads
    me = lax.axis_index("seq")
    seg = lax.axis_index("seg")
    owner = lax.rem(me, span) == 0
    mine = me // span

    barrier = pltpu.get_barrier_semaphore()
    for d in range(1, seqs):
        pl.semaphore_signal(
            barrier, inc=1,
            device_id={"seq": lax.rem(me + d, seqs), "seg": seg}, device_id_type=MESH,
        )
    for d in range(1, segs):
        pl.semaphore_signal(
            barrier, inc=1,
            device_id={"seq": me, "seg": lax.rem(seg + d, segs)}, device_id_type=MESH,
        )

    def copy(src, dst, put, got, to_seq, to_seg):
        return pltpu.make_async_remote_copy(
            src_ref=src, dst_ref=dst, send_sem=put, recv_sem=got,
            device_id={"seq": to_seq, "seg": to_seg}, device_id_type=MESH,
        )

    def put(h):
        return copy(pair.at[h], rx.at[me], put_sem.at[h], got_sem.at[me], h * span, seg)

    def got(s):
        return copy(rx.at[s], rx.at[s], put_sem.at[0], got_sem.at[s], s, seg)

    def sput(s):
        return copy(outgoing.at[s], own_state.at[mine], sput_sem.at[s], sgot_sem.at[mine], s, seg)

    def sgot(h):
        return copy(outgoing.at[0], own_state.at[h], sput_sem.at[0], sgot_sem.at[h], h * span, seg)

    def zput(g):
        return copy(tree.at[seqs - 2], zx.at[seg], zput_sem.at[g], zgot_sem.at[seg], me, g)

    def zgot(g):
        return copy(tree.at[seqs - 2], zx.at[g], zput_sem.at[g], zgot_sem.at[g], me, g)

    def fput(g):
        return copy(first_state, zstate, zput_sem.at[g], zgot_sem.at[0], me, g)

    kf[...] = k_ref[...].astype(F32)
    vf[...] = v_ref[...].astype(F32)
    qf[...] = q_ref[...].astype(F32)

    def local(i, _):
        turn = lax.rem(i + 1 + mine // per, heads // per)
        factors(turn * per, per, heads, nblk, kf, vf, dsc, nsc, kb, scaled_hi, scaled_lo, before, pair)

        @pl.when(i == 0)
        def _():
            pl.semaphore_wait(barrier, seqs + segs - 2)

        for d in range(per):
            h = turn * per + d

            @pl.when(me != h * span)
            def _():
                put(h).start()

        return 0

    lax.fori_loop(0, heads // per, local, 0)

    def reading(h, _):
        readers(h, heads, nblk, qf, kb, scaled_hi, scaled_lo, before, reach, base)
        return 0

    lax.fori_loop(0, heads, reading, 0)

    @pl.when(owner)
    def _():
        total[:, :dk] = jnp.where(iota((dk, dk), 0) == iota((dk, dk), 1), 1.0, 0.0).astype(F32)
        total[:, dk:] = jnp.zeros((dk, dv), F32)
        rx[me] = pair[mine]

        def arrived(s, _):
            @pl.when(s != me)
            def _():
                got(s).wait_recv()

            return 0

        lax.fori_loop(0, seqs, arrived, 0)
        parts = [rx.at[s] for s in range(seqs)]
        slot = 0
        while len(parts) > 1:
            joined = []
            for early, late in zip(parts[::2], parts[1::2]):
                after = dot3(split(late[:, :dk]), split(early[...]))
                tree[slot, :, :dk] = after[:, :dk]
                tree[slot, :, dk:] = after[:, dk:] + late[:, dk:]
                joined.append(tree.at[slot])
                slot += 1
            parts = joined + (parts[-1:] if len(parts) % 2 else [])

        @pl.when(seg == 0)
        def _():
            whole = tree[seqs - 2]
            first_state[...] = dot3(split(whole[:, :dk]), split(init_ref[mine])) + whole[:, dk:]
            for g in range(1, segs):
                fput(g).start()

        for g in range(2, segs):

            @pl.when((seg > 0) & (seg < g))
            def _():
                zput(g).start()

        def one(s, _):
            so_far = total[...]
            prefix[s] = so_far
            after = dot3(split(rx[s, :, :dk]), split(so_far))
            total[:, :dk] = after[:, :dk]
            total[:, dk:] = after[:, dk:] + rx[s, :, dk:]
            return 0

        lax.fori_loop(0, seqs, one, 0)

    @pl.when(owner)
    def _():
        @pl.when(seg == 0)
        def _():
            state[...] = init_ref[mine]

        @pl.when(seg > 0)
        def _():
            fput(0).wait_recv()
            state[...] = zstate[...]

        for g in range(1, segs - 1):

            @pl.when(g < seg)
            def _():
                zgot(g).wait_recv()
                state[...] = dot3(split(zx[g, :, :dk]), split(state[...])) + zx[g, :, dk:]

        def give(k, _):
            s = lax.rem(2 * seqs - 2 - me + k, seqs)
            ready = dot3(split(prefix[s, :, :dk]), split(state[...])) + prefix[s, :, dk:]

            @pl.when(s != me)
            def _():
                outgoing[s] = ready
                sput(s).start()

            @pl.when(s == me)
            def _():
                own_state[mine] = ready

            return 0

        lax.fori_loop(0, seqs, give, 0)

    for h in range(heads):

        @pl.when(me != h * span)
        def _():
            sgot(h).wait_recv()

        read = dot3(split(reach[h]), split(own_state[h])) + base[h]
        scale = lax.rsqrt(jnp.mean(read * read, axis=-1, keepdims=True) + 1e-6)
        normed = read * scale * gain_ref[h : h + 1, :]
        qf[pl.ds(h, read.shape[0], stride=heads), :] = normed
    out_ref[...] = qf[...].astype(BF16)

    for h in range(heads):

        @pl.when(me != h * span)
        def _():
            put(h).wait_send()

    @pl.when(owner)
    def _():
        @pl.when(seg == 0)
        def _():
            for g in range(1, segs):
                fput(g).wait_send()

        for g in range(2, segs):

            @pl.when((seg > 0) & (seg < g))
            def _():
                zput(g).wait_send()

        def done(s, _):
            @pl.when(s != me)
            def _():
                sput(s).wait_send()

            return 0

        lax.fori_loop(0, seqs, done, 0)


def per_device(seqs, segs, query_rows, key_rows, value_rows, out_gain, initial_state):
    _, tokens, heads, dk = query_rows.shape
    dv = value_rows.shape[-1]
    steps = tokens * REFL
    nblk = steps // BLK
    per = 2
    count = per * nblk
    wide = dk + dv
    vmem = pl.BlockSpec(memory_space=pltpu.VMEM)
    dma = pltpu.SemaphoreType.DMA
    out = pl.pallas_call(
        functools.partial(kernel, seqs, segs, heads, per),
        in_specs=[vmem] * 5,
        out_specs=vmem,
        out_shape=jax.ShapeDtypeStruct((tokens * heads, dv), BF16),
        scratch_shapes=[
            pltpu.VMEM((tokens * heads, dk), F32),
            pltpu.VMEM((steps * heads, dk), F32),
            pltpu.VMEM((steps * heads, dv), F32),
            pltpu.VMEM((count * SUB, BLK), F32),
            pltpu.VMEM((count * SUB, BLK), F32),
            pltpu.VMEM((heads, nblk, BLK, dk), BF16),
            pltpu.VMEM((heads, nblk, BLK, wide), BF16),
            pltpu.VMEM((heads, nblk, BLK, wide), BF16),
            pltpu.VMEM((heads, nblk, dk, wide), F32),
            pltpu.VMEM((heads, dk, wide), F32),
            pltpu.VMEM((heads, tokens, dk), F32),
            pltpu.VMEM((heads, tokens, dv), F32),
            pltpu.VMEM((seqs, dk, wide), F32),
            pltpu.VMEM((seqs, dk, wide), F32),
            pltpu.VMEM((seqs, dk, dv), F32),
            pltpu.VMEM((dk, wide), F32),
            pltpu.VMEM((seqs - 1, dk, wide), F32),
            pltpu.VMEM((segs, dk, wide), F32),
            pltpu.VMEM((dk, dv), F32),
            pltpu.VMEM((dk, dv), F32),
            pltpu.VMEM((heads, dk, dv), F32),
            pltpu.VMEM((dk, dv), F32),
            dma((heads,)),
            dma((seqs,)),
            dma((segs,)),
            dma((segs,)),
            dma((seqs,)),
            dma((heads,)),
        ],
        compiler_params=pltpu.CompilerParams(collective_id=0, has_side_effects=True),
        name="delta_product",
    )(
        query_rows.reshape(tokens * heads, dk),
        key_rows.reshape(steps * heads, dk),
        value_rows.reshape(steps * heads, dv),
        out_gain,
        initial_state,
    )
    return out.reshape(1, tokens, heads, dv)


def solution(mesh):
    return jax.shard_map(
        functools.partial(per_device, mesh.shape["seq"], mesh.shape["seg"]),
        mesh=mesh,
        in_specs=(
            P("seg", "seq", None, None),
            P("seg", "seq", None, None, None),
            P("seg", "seq", None, None, None),
            P(),
            P(),
        ),
        out_specs=P("seg", "seq", None, None),
        check_vma=False,
    )
```

```python
import functools

import jax
import jax.numpy as jnp
from jax import lax
from jax.experimental import pallas as pl
from jax.experimental.pallas import tpu as pltpu
from jax.sharding import PartitionSpec as P

F32 = jnp.float32
BF16 = jnp.bfloat16
REFL = 2
BLK = 128
SUB = 16
LANES = 128
MESH = pl.DeviceIdType.MESH


def dot(a, b):
    return lax.dot_general(a, b, (((1,), (0,)), ((), ())), preferred_element_type=F32)


def dot_bt(a, b):
    return lax.dot_general(a, b, (((1,), (1,)), ((), ())), preferred_element_type=F32)


def dot_at(a, b):
    return lax.dot_general(a, b, (((0,), (0,)), ((), ())), preferred_element_type=F32)


def split(x):
    high = x.astype(BF16)
    return high, (x - high.astype(F32)).astype(BF16)


def dot3(a, b):
    ah, al = a
    bh, bl = b
    rows, width = ah.shape[0], bh.shape[1]
    both = jnp.concatenate([ah, al], 0)
    if width <= LANES:
        full = dot(both, jnp.concatenate([bh, bl], 1))
        return full[:rows, :width] + (full[:rows, width:] + full[rows:, :width])
    full = dot(both, bh)
    return full[:rows] + (full[rows:] + dot(ah, bl))


def dot2(a, exact):
    rows = a[0].shape[0]
    full = dot(jnp.concatenate(a, 0), exact)
    return full[:rows] + full[rows:]


def iota(shape, axis):
    return lax.broadcasted_iota(jnp.int32, shape, axis)


def grouped(x, size, odd):
    return [x[g * size : (g + 1) * size] for g in range(odd, x.shape[0] // size, 2)]


def factors(first, per, heads, nblk, kf, vf, dsc, nsc, kb, scaled_hi, scaled_lo, before, pair):
    dk = kf.shape[1]
    row, col = iota((BLK, BLK), 0), iota((BLK, BLK), 1)
    eye = row == col
    lane = iota((SUB, BLK), 1)
    count = per * nblk

    keys, lowers, rcols, rrows = [], [], [], []
    for n in range(count):
        h, c = n // nblk, n % nblk
        key = kf[pl.ds(c * BLK * heads + first + h, BLK, stride=heads), :].astype(BF16)
        kb[first + h, c] = key
        gram = dot_bt(key, key)
        diag = jnp.where(eye, gram, 0.0)
        rcol = lax.rsqrt(jnp.sum(diag, axis=1, keepdims=True) + 1e-6)
        rrow = lax.rsqrt(jnp.sum(diag, axis=0, keepdims=True) + 1e-6)
        lower = jnp.where(row > col, gram * (2.0 * rcol) * rrow, 0.0)
        packed = lower[:SUB]
        for g in range(1, BLK // SUB):
            packed = jnp.where(lane // SUB == g, lower[g * SUB : (g + 1) * SUB], packed)
        dsc[n * SUB : (n + 1) * SUB, :] = packed
        keys.append(key)
        lowers.append(lower)
        rcols.append(rcol)
        rrows.append(rrow)

    lane_c = iota((count, BLK), 1)
    solved = []
    for i in range(SUB):
        line = dsc[pl.ds(i, count, stride=SUB), :]
        total = jnp.where(lane_c % SUB == i, 1.0, 0.0)
        for j in range(i):
            factor = jnp.take_along_axis(line, (lane_c // SUB) * SUB + j, axis=1)
            total = total - factor * solved[j]
        solved.append(total)
        nsc[pl.ds(i, count, stride=SUB), :] = total

    inverses = []
    for n in range(count):
        packed = nsc[n * SUB : (n + 1) * SUB, :]
        inverses.append(
            jnp.concatenate(
                [jnp.where(lane // SUB == g, packed, 0.0) for g in range(BLK // SUB)], axis=0
            )
        )
    half = BLK // 2
    size = SUB
    while size < BLK:
        paired = iota((half, BLK), 1) // size == 2 * (iota((half, BLK), 0) // size)
        for n in range(count):
            inv = split(inverses[n])
            odd = jnp.concatenate(grouped(lowers[n], size, 1), 0)
            part = dot3(split(jnp.where(paired, odd, 0.0)), inv)
            blank = jnp.zeros((size, BLK), F32)
            spread = []
            for g in range(half // size):
                spread += [blank, part[g * size : (g + 1) * size]]
            own = tuple(jnp.concatenate(grouped(x, size, 1), 0) for x in inv)
            fill = dot3(own, split(jnp.concatenate(spread, 0)))
            even, odd = grouped(inverses[n], size, 0), grouped(inverses[n], size, 1)
            rows = []
            for g in range(half // size):
                rows += [even[g], odd[g] - fill[g * size : (g + 1) * size]]
            inverses[n] = jnp.concatenate(rows, 0)
        size *= 2

    for h in range(per):
        trans = add = None
        for c in range(nblk):
            n = h * nblk + c
            key, rcol, rrow = keys[n], rcols[n], rrows[n]
            value = vf[pl.ds(c * BLK * heads + first + h, BLK, stride=heads), :].astype(BF16)
            weights = dot2(split(inverses[n] * (2.0 * rrow)), key)
            updates = dot2(split(inverses[n] * 2.0), value)
            scaled = split(jnp.concatenate([weights, updates], axis=1) * rcol)
            scaled_hi[first + h, c] = scaled[0]
            scaled_lo[first + h, c] = scaled[1]
            moved = dot_at(key, scaled[0]) + dot_at(key, scaled[1])
            step_trans = jnp.where(eye, 1.0, 0.0) - moved[:, :dk]
            step_add = moved[:, dk:]
            if c == 0:
                trans, add = step_trans, step_add
            else:
                so_far = jnp.concatenate([trans, add], axis=1)
                before[first + h, c] = so_far
                after = dot3(split(step_trans), split(so_far))
                trans, add = after[:, :dk], after[:, dk:] + step_add
        pair[first + h, :, :dk] = trans
        pair[first + h, :, dk:] = add


def readers(h, heads, nblk, qf, kb, scaled_hi, scaled_lo, before, reach, base):
    dk = qf.shape[1]
    tok = BLK // REFL
    visible = iota((tok, BLK), 1) <= REFL * iota((tok, BLK), 0) + (REFL - 1)
    for c in range(nblk):
        query = qf[pl.ds(c * tok * heads + h, tok, stride=heads), :]
        scores = jnp.where(visible, dot_bt(query.astype(BF16), kb[h, c]), 0.0)
        read = dot3(split(scores), (scaled_hi[h, c], scaled_lo[h, c]))
        project = query - read[:, :dk]
        local = read[:, dk:]
        rows = slice(c * tok, (c + 1) * tok)
        if c == 0:
            reach[h, rows, :] = project
            base[h, rows, :] = local
        else:
            gone = dot3(split(project), split(before[h, c]))
            reach[h, rows, :] = gone[:, :dk]
            base[h, rows, :] = gone[:, dk:] + local


def kernel(
    seqs, segs, heads, per,
    q_ref, k_ref, v_ref, gain_ref, init_ref, out_ref,
    qf, kf, vf, dsc, nsc, kb, scaled_hi, scaled_lo, before, pair, reach, base,
    rx, prefix, outgoing, total, tree, zx, first_state, zstate, own_state, state,
    put_sem, got_sem, zput_sem, zgot_sem, sput_sem, sgot_sem,
):
    dk = init_ref.shape[1]
    dv = init_ref.shape[2]
    nblk = k_ref.shape[0] // (heads * BLK)
    span = seqs // heads
    me = lax.axis_index("seq")
    seg = lax.axis_index("seg")
    owner = lax.rem(me, span) == 0
    mine = me // span

    barrier = pltpu.get_barrier_semaphore()
    for d in range(1, seqs):
        pl.semaphore_signal(
            barrier, inc=1,
            device_id={"seq": lax.rem(me + d, seqs), "seg": seg}, device_id_type=MESH,
        )
    for d in range(1, segs):
        pl.semaphore_signal(
            barrier, inc=1,
            device_id={"seq": me, "seg": lax.rem(seg + d, segs)}, device_id_type=MESH,
        )

    def copy(src, dst, put, got, to_seq, to_seg):
        return pltpu.make_async_remote_copy(
            src_ref=src, dst_ref=dst, send_sem=put, recv_sem=got,
            device_id={"seq": to_seq, "seg": to_seg}, device_id_type=MESH,
        )

    def put(h):
        return copy(pair.at[h], rx.at[me], put_sem.at[h], got_sem.at[me], h * span, seg)

    def got(s):
        return copy(rx.at[s], rx.at[s], put_sem.at[0], got_sem.at[s], s, seg)

    def sput(s):
        return copy(outgoing.at[s], own_state.at[mine], sput_sem.at[s], sgot_sem.at[mine], s, seg)

    def sgot(h):
        return copy(outgoing.at[0], own_state.at[h], sput_sem.at[0], sgot_sem.at[h], h * span, seg)

    def zput(g):
        return copy(tree.at[seqs - 2], zx.at[seg], zput_sem.at[g], zgot_sem.at[seg], me, g)

    def zgot(g):
        return copy(tree.at[seqs - 2], zx.at[g], zput_sem.at[g], zgot_sem.at[g], me, g)

    def fput(g):
        return copy(first_state, zstate, zput_sem.at[g], zgot_sem.at[0], me, g)

    kf[...] = k_ref[...].astype(F32)
    vf[...] = v_ref[...].astype(F32)
    qf[...] = q_ref[...].astype(F32)

    def local(i, _):
        turn = lax.rem(i + 1 + mine // per, heads // per)
        if heads == 4 and per == 1:
            left = heads - 1 - i
            row, col = lax.rem(mine // 2 + left // 2, 2), lax.rem(mine + left, 2)
            turn = 2 * row + col
        factors(turn * per, per, heads, nblk, kf, vf, dsc, nsc, kb, scaled_hi, scaled_lo, before, pair)

        @pl.when(i == 0)
        def _():
            pl.semaphore_wait(barrier, seqs + segs - 2)

        for d in range(per):
            h = turn * per + d

            @pl.when(me != h * span)
            def _():
                put(h).start()

        return 0

    lax.fori_loop(0, heads // per, local, 0)

    def reading(h, _):
        readers(h, heads, nblk, qf, kb, scaled_hi, scaled_lo, before, reach, base)
        return 0

    lax.fori_loop(0, heads, reading, 0)

    @pl.when(owner)
    def _():
        total[:, :dk] = jnp.where(iota((dk, dk), 0) == iota((dk, dk), 1), 1.0, 0.0).astype(F32)
        total[:, dk:] = jnp.zeros((dk, dv), F32)
        rx[me] = pair[mine]

        def arrived(s, _):
            @pl.when(s != me)
            def _():
                got(s).wait_recv()

            return 0

        lax.fori_loop(0, seqs, arrived, 0)
        parts = [rx.at[s] for s in range(seqs)]
        slot = 0
        while len(parts) > 1:
            joined = []
            for early, late in zip(parts[::2], parts[1::2]):
                after = dot3(split(late[:, :dk]), split(early[...]))
                tree[slot, :, :dk] = after[:, :dk]
                tree[slot, :, dk:] = after[:, dk:] + late[:, dk:]
                joined.append(tree.at[slot])
                slot += 1
            parts = joined + (parts[-1:] if len(parts) % 2 else [])

        @pl.when(seg == 0)
        def _():
            whole = tree[seqs - 2]
            first_state[...] = dot3(split(whole[:, :dk]), split(init_ref[mine])) + whole[:, dk:]
            for g in range(1, segs):
                fput(g).start()

        for g in range(2, segs):

            @pl.when((seg > 0) & (seg < g))
            def _():
                zput(g).start()

        def one(s, _):
            so_far = total[...]
            prefix[s] = so_far
            after = dot3(split(rx[s, :, :dk]), split(so_far))
            total[:, :dk] = after[:, :dk]
            total[:, dk:] = after[:, dk:] + rx[s, :, dk:]
            return 0

        lax.fori_loop(0, seqs, one, 0)

    @pl.when(owner)
    def _():
        @pl.when(seg == 0)
        def _():
            state[...] = init_ref[mine]

        @pl.when(seg > 0)
        def _():
            fput(0).wait_recv()
            state[...] = zstate[...]

        for g in range(1, segs - 1):

            @pl.when(g < seg)
            def _():
                zgot(g).wait_recv()
                state[...] = dot3(split(zx[g, :, :dk]), split(state[...])) + zx[g, :, dk:]

        def give(k, _):
            s = lax.rem(2 * seqs - 2 - me + k, seqs)
            ready = dot3(split(prefix[s, :, :dk]), split(state[...])) + prefix[s, :, dk:]

            @pl.when(s != me)
            def _():
                outgoing[s] = ready
                sput(s).start()

            @pl.when(s == me)
            def _():
                own_state[mine] = ready

            return 0

        lax.fori_loop(0, seqs, give, 0)

    for h in range(heads):

        @pl.when(me != h * span)
        def _():
            sgot(h).wait_recv()

        read = dot3(split(reach[h]), split(own_state[h])) + base[h]
        scale = lax.rsqrt(jnp.mean(read * read, axis=-1, keepdims=True) + 1e-6)
        normed = read * scale * gain_ref[h : h + 1, :]
        qf[pl.ds(h, read.shape[0], stride=heads), :] = normed
    out_ref[...] = qf[...].astype(BF16)

    for h in range(heads):

        @pl.when(me != h * span)
        def _():
            put(h).wait_send()

    @pl.when(owner)
    def _():
        @pl.when(seg == 0)
        def _():
            for g in range(1, segs):
                fput(g).wait_send()

        for g in range(2, segs):

            @pl.when((seg > 0) & (seg < g))
            def _():
                zput(g).wait_send()

        def done(s, _):
            @pl.when(s != me)
            def _():
                sput(s).wait_send()

            return 0

        lax.fori_loop(0, seqs, done, 0)


def per_device(seqs, segs, query_rows, key_rows, value_rows, out_gain, initial_state):
    _, tokens, heads, dk = query_rows.shape
    dv = value_rows.shape[-1]
    steps = tokens * REFL
    nblk = steps // BLK
    per = 1
    count = per * nblk
    wide = dk + dv
    vmem = pl.BlockSpec(memory_space=pltpu.VMEM)
    dma = pltpu.SemaphoreType.DMA
    out = pl.pallas_call(
        functools.partial(kernel, seqs, segs, heads, per),
        in_specs=[vmem] * 5,
        out_specs=vmem,
        out_shape=jax.ShapeDtypeStruct((tokens * heads, dv), BF16),
        scratch_shapes=[
            pltpu.VMEM((tokens * heads, dk), F32),
            pltpu.VMEM((steps * heads, dk), F32),
            pltpu.VMEM((steps * heads, dv), F32),
            pltpu.VMEM((count * SUB, BLK), F32),
            pltpu.VMEM((count * SUB, BLK), F32),
            pltpu.VMEM((heads, nblk, BLK, dk), BF16),
            pltpu.VMEM((heads, nblk, BLK, wide), BF16),
            pltpu.VMEM((heads, nblk, BLK, wide), BF16),
            pltpu.VMEM((heads, nblk, dk, wide), F32),
            pltpu.VMEM((heads, dk, wide), F32),
            pltpu.VMEM((heads, tokens, dk), F32),
            pltpu.VMEM((heads, tokens, dv), F32),
            pltpu.VMEM((seqs, dk, wide), F32),
            pltpu.VMEM((seqs, dk, wide), F32),
            pltpu.VMEM((seqs, dk, dv), F32),
            pltpu.VMEM((dk, wide), F32),
            pltpu.VMEM((seqs - 1, dk, wide), F32),
            pltpu.VMEM((segs, dk, wide), F32),
            pltpu.VMEM((dk, dv), F32),
            pltpu.VMEM((dk, dv), F32),
            pltpu.VMEM((heads, dk, dv), F32),
            pltpu.VMEM((dk, dv), F32),
            dma((heads,)),
            dma((seqs,)),
            dma((segs,)),
            dma((segs,)),
            dma((seqs,)),
            dma((heads,)),
        ],
        compiler_params=pltpu.CompilerParams(collective_id=0, has_side_effects=True),
        name="delta_product",
    )(
        query_rows.reshape(tokens * heads, dk),
        key_rows.reshape(steps * heads, dk),
        value_rows.reshape(steps * heads, dv),
        out_gain,
        initial_state,
    )
    return out.reshape(1, tokens, heads, dv)


def solution(mesh):
    return jax.shard_map(
        functools.partial(per_device, mesh.shape["seq"], mesh.shape["seg"]),
        mesh=mesh,
        in_specs=(
            P("seg", "seq", None, None),
            P("seg", "seq", None, None, None),
            P("seg", "seq", None, None, None),
            P(),
            P(),
        ),
        out_specs=P("seg", "seq", None, None),
        check_vma=False,
    )
```
